512 devices in a mesh: rep: 64 (over z, y_lo, core), voc: 8 (over y_hi, x).
Axes of the slice: x: 4, y: 8 (y_hi: 2, y_lo: 4; y = y_hi * 4 + y_lo), z: 8, core: 2. Of those that a mesh axis runs over, the one named last changes fastest.
Arguments:
- states: bfloat16 [2, 256, 24576], P(None, None, 'rep'), may hold values from -6 to 6
- head_weight: bfloat16 [24576, 16384], P('rep', 'voc'), may hold values from -0.21875 to 0.21875
- pair_order: int32 [2, 32], replicated, may hold values from 0 to 31, each once within a row
- row_example: int32 [2, 32, 256], replicated, may hold values from 0 to 255, each once within a row
Outputs:
- state_grad: bfloat16 [2, 256, 24576], P(None, None, 'rep')
- head_grad: bfloat16 [24576, 16384], P('rep', 'voc')
The draws below stay inside these ranges and needn't reach their ends.
Inputs may be any that keep to these rules, and one draw needn't show every extreme that they name: Each row pair_order[m] holds every replica once. Each row row_example[m, r] holds every number of 0 to 255 once.
All inputs are finite; a program needn't handle non-finite values.
Results may differ from the reference program's by a relative error of at most 0.0055.
Values may be sent and summed in bfloat16 or wider, within the bound.
A program may use at most 64 MiB of HBM per device.

```python
import jax
import jax.numpy as jnp
from jax import lax

D = 768
MB = 2
B = 256
REPLICAS = 32
V = 16384


def levels(stream_key, dims, pieces, low, largest):
    loudness = 1.0
    for dim, parts in pieces:
        steps = jax.random.uniform(jax.random.fold_in(jax.random.fold_in(stream_key, 6), dim), (parts,), jnp.float32, low / len(pieces), largest / len(pieces))
        loudness = loudness * jnp.repeat(jnp.exp(steps), dims[dim] // parts).reshape((-1,) + (1,) * (len(dims) - 1 - dim))
    return loudness


def scatter_about(rng, dims, deviation, limit, shards=(), kind=jnp.bfloat16):
    result = jax.random.normal(rng, dims, jnp.float32) * deviation
    if len(shards) > 0:
        result = levels(rng, dims, shards, -0.22, 0.18) * result
    return jnp.clip(result, min=-limit, max=limit).astype(kind)


def setup_inputs(seed: int = 0) -> dict:
    keys = jax.random.split(jax.random.key(seed), 5)
    states = scatter_about(keys[0], (MB, B, REPLICAS * D), 1.0, 6.0, ((2, 64),))
    head_weight = scatter_about(keys[1], (REPLICAS * D, V), D ** -0.5, 0.21875, ((0, 64), (1, 8)))
    pair_order = jax.vmap(lambda own: jax.random.permutation(own, REPLICAS))(jax.random.split(keys[2], MB)).reshape((MB, REPLICAS)).astype(jnp.int32)
    row_example = jax.vmap(lambda own: jax.random.permutation(own, B))(jax.random.split(keys[3], MB * REPLICAS)).reshape((MB, REPLICAS, B)).astype(jnp.int32)
    return {"states": states, "head_weight": head_weight, "pair_order": pair_order, "row_example": row_example}


distill_weight = 0.0625


def partner_table(pair_order):
    slot_count = pair_order.shape[1]
    slot_ids = jnp.arange(slot_count, dtype=jnp.int32)
    matches = pair_order[:, None, :] == slot_ids[None, :, None]
    position = jnp.sum(jnp.where(matches, slot_ids[None, None, :], 0), axis=2).astype(jnp.int32)
    following = ((position + 1) % slot_count).astype(jnp.int32)
    return jnp.take_along_axis(pair_order, following, axis=1)


def to_examples(rows_in, examples):
    slot_count = examples.shape[1]
    slot_ids = jnp.arange(slot_count, dtype=jnp.int32)
    onehot = (examples[:, None, :] == slot_ids[None, :, None]).astype(jnp.float32)
    return jnp.einsum("mei,miw->mew", onehot, rows_in.astype(jnp.float32)).astype(jnp.bfloat16)


def reference(states, head_weight, pair_order, row_example):
    micro_count, row_count, total_width = states.shape
    replica_count = pair_order.shape[1]
    width = total_width // replica_count
    vocab = head_weight.shape[1]
    partner = partner_table(pair_order)
    micro_ids = jnp.arange(micro_count, dtype=jnp.int32)

    def pieces_of(replica):
        block = lax.dynamic_slice_in_dim(states, replica * width, width, 2)
        weights = lax.dynamic_slice_in_dim(head_weight, replica * width, width, 0)
        examples = lax.dynamic_index_in_dim(row_example, replica, 1, keepdims=False)
        return to_examples(block, examples), weights, examples

    def logits_of(replica):
        ordered, weights, examples = pieces_of(replica)
        flat = jnp.dot(ordered.reshape(-1, width), weights, preferred_element_type=jnp.float32)
        return flat.astype(jnp.bfloat16).reshape(micro_count, row_count, vocab)

    replica_ids = jnp.arange(replica_count, dtype=jnp.int32)
    logits = lax.map(logits_of, replica_ids)

    def grads_of(replica):
        ordered, weights, examples = pieces_of(replica)
        own_logits = logits[replica]
        mates = partner[:, replica]
        mate_logits = logits[mates, micro_ids]
        gradient = (distill_weight * (own_logits.astype(jnp.float32) - mate_logits.astype(jnp.float32))).astype(jnp.bfloat16)
        flat_grad = gradient.reshape(-1, vocab)
        head_part = jnp.dot(ordered.reshape(-1, width).T, flat_grad, preferred_element_type=jnp.float32).astype(jnp.bfloat16)
        example_grad = jnp.dot(flat_grad, weights.T, preferred_element_type=jnp.float32).astype(jnp.bfloat16)
        example_grad = example_grad.reshape(micro_count, row_count, width)
        state_part = jnp.take_along_axis(example_grad, examples[:, :, None], axis=1)
        return state_part, head_part

    state_parts, head_parts = lax.map(grads_of, replica_ids)
    state_grad = state_parts.transpose(1, 2, 0, 3).reshape(micro_count, row_count, replica_count * width)
    head_grad = head_parts.reshape(replica_count * width, vocab)
    return state_grad, head_grad
```

```python
import functools

import jax
import jax.numpy as jnp
from jax import lax
from jax.experimental import pallas as pl
from jax.experimental.pallas import tpu as pltpu
from jax.sharding import PartitionSpec as P

MESH = pl.DeviceIdType.MESH
SCALE = 0.0625
F32, BF16 = jnp.float32, jnp.bfloat16


def kernel(
    dims,
    pair_order,
    states_hbm,
    weight_hbm,
    example_hbm,
    state_hbm,
    head_hbm,
    weight,
    weight_t,
    states,
    examples,
    onehot,
    ordered,
    ordered_t,
    mine,
    sent,
    got,
    logits,
    pool_0,
    pool_1,
    spread,
    grad,
    part,
    part_b,
    xin,
    half,
    half_in,
    total,
    state_out,
    head_out,
    partner,
    in_sem,
    out_sem,
    pair_send,
    pair_recv,
    one_send,
    one_recv,
    two_send,
    two_recv,
    fwd_send,
    fwd_recv,
    xs_send,
    xs_recv,
    y_send,
    y_recv,
    xg_send,
    xg_recv,
):
    NZ, NY, NX, NH = dims
    pools = (pool_0, pool_1)
    mb, rows, width = states.shape
    vocab = weight.shape[1]
    count = NZ * NY
    side_rows = rows // 2
    chunk = side_rows // 2
    rg, cg = side_rows // NZ, vocab // NY
    zh = NZ // 2
    quarter = rows // NX

    rep, voc = lax.axis_index("rep"), lax.axis_index("voc")
    core = lax.rem(rep, 2)
    rid = rep // 2
    z, y = rid // NY, lax.rem(rid, NY)
    h, x = voc // NX, lax.rem(voc, NX)
    slot_of = lambda zz, yy: yy * NZ + lax.rem(zz, 2) * zh + zz // 2
    my_slot = slot_of(z, y)
    pair = {"rep": rid * 2 + 1 - core}
    across = {"voc": (NH - 1 - h) * NX + x}

    loads = [
        pltpu.make_async_copy(example_hbm, examples, in_sem.at[0]),
        pltpu.make_async_copy(states_hbm, states, in_sem.at[1]),
        pltpu.make_async_copy(weight_hbm, weight, in_sem.at[2]),
    ]
    for load in loads:
        load.start()

    barrier = pltpu.get_barrier_semaphore()

    @pl.loop(0, count)
    def _(k):
        @pl.when(k != rid)
        def _():
            pl.semaphore_signal(barrier, inc=1, device_id={"rep": k * 2 + core}, device_id_type=MESH)

    pl.semaphore_signal(barrier, inc=1, device_id=pair, device_id_type=MESH)
    for k in range(1, NX):
        pl.semaphore_signal(
            barrier, inc=1, device_id={"voc": h * NX + lax.rem(x + k, NX)}, device_id_type=MESH
        )
    if NH > 1:
        pl.semaphore_signal(barrier, inc=1, device_id=across, device_id_type=MESH)

    loads[0].wait()
    loads[1].wait()
    ids = lax.broadcasted_iota(jnp.int32, (rows, rows), 0)
    for m in range(mb):
        row = examples[m, pl.ds(rid, 1), :]
        onehot[m] = (ids == row).astype(BF16)
        ordered[m] = jnp.dot(onehot[m], states[m], preferred_element_type=F32).astype(BF16)
    loads[2].wait()

    def partials(side, target):
        at = pl.multiple_of(side * side_rows, side_rows)
        left = jnp.concatenate([ordered[m, pl.ds(at, side_rows), :] for m in range(mb)], axis=0)

        @pl.loop(0, NY)
        def _(j):
            cols = pl.ds(pl.multiple_of(j * cg, cg), cg)
            out = jnp.dot(left, weight[:, cols], preferred_element_type=F32)
            for m in range(mb):
                for u in range(2):
                    lo = m * side_rows + u * chunk
                    target[m, u, :, cols] = out[lo : lo + chunk]

    partials(1 - core, sent)
    pl.semaphore_wait(barrier, count - 1 + 1 + NX - 1 + (1 if NH > 1 else 0))

    def pair_copy(m, u):
        return pltpu.make_async_remote_copy(
            src_ref=sent.at[m, u],
            dst_ref=got.at[m, u],
            send_sem=pair_send.at[m, u],
            recv_sem=pair_recv.at[m, u],
            device_id=pair,
            device_id_type=MESH,
        )

    for m in range(mb):
        for u in range(2):
            pair_copy(m, u).start()
    partials(core, mine)

    for m in range(mb):
        for u in range(2):
            pair_copy(m, u).wait_recv()

            @pl.loop(0, NY)
            def _(j):
                cols = pl.ds(pl.multiple_of(j * cg, cg), cg)
                both = (mine[m, u, :, cols] + got[m, u, :, cols]).astype(BF16)
                logits[m, pl.ds(j * NZ + u * zh, zh)] = both.reshape(zh, rg, cg)

            @pl.loop(0, zh * NY)
            def _(k):
                zt = u + 2 * lax.rem(z // 2 + k // NY, zh)
                yt = lax.rem(y + lax.rem(k, NY), NY)
                target = zt * NY + yt
                src, dst = logits.at[m, slot_of(zt, yt)], pools[m].at[rid]

                @pl.when(target != rid)
                def _():
                    pltpu.make_async_remote_copy(
                        src_ref=src,
                        dst_ref=dst,
                        send_sem=one_send.at[m],
                        recv_sem=one_recv.at[m],
                        device_id={"rep": target * 2 + core},
                        device_id_type=MESH,
                    ).start()

                @pl.when(target == rid)
                def _():
                    pltpu.make_async_copy(src, dst, one_recv.at[m]).start()

    for m in range(mb):

        @pl.loop(0, count)
        def _(r):
            found = jnp.int32(0)
            for k in range(count):
                found += jnp.where(pair_order[m, k] == r, pair_order[m, (k + 1) % count], 0)
            partner[m, r] = found

        ordered_t[m] = ordered[m].T

    @pl.loop(0, NY)
    def _(j):
        at = pl.multiple_of(j * cg, cg)
        weight_t[pl.ds(at, cg), :] = weight[:, pl.ds(at, cg)].T

    for m in range(mb):
        pool = pools[m]
        pltpu.make_async_copy(pool, pool, one_recv.at[m]).wait()

        def place(k):
            return lax.rem(z + k // NY, NZ) * NY + lax.rem(y + lax.rem(k, NY), NY)

        @pl.loop(0, count // 4)
        def _(b):
            for i in range(4):
                r = place(b * 4 + i)
                own, other = pool[r], pool[partner[m, r]]
                spread[m, r] = (SCALE * (own.astype(F32) - other.astype(F32))).astype(BF16)
            for i in range(4):
                r = place(b * 4 + i)
                src, dst = spread.at[m, r], grad.at[m, core, my_slot]

                @pl.when(r != rid)
                def _():
                    pltpu.make_async_remote_copy(
                        src_ref=src,
                        dst_ref=dst,
                        send_sem=two_send.at[m],
                        recv_sem=two_recv.at[m],
                        device_id={"rep": r * 2 + core},
                        device_id_type=MESH,
                    ).start()

                @pl.when(r == rid)
                def _():
                    pltpu.make_async_copy(src, dst, two_recv.at[m]).start()

    def forward(m):
        return pltpu.make_async_remote_copy(
            src_ref=grad.at[m, core],
            dst_ref=grad.at[m, core],
            send_sem=fwd_send.at[m],
            recv_sem=fwd_recv.at[m],
            device_id=pair,
            device_id_type=MESH,
        )

    def scatter(m, k):
        xt = lax.rem(x + k, NX)
        return pltpu.make_async_remote_copy(
            src_ref=part_b.at[m, xt],
            dst_ref=xin.at[m, x],
            send_sem=xs_send.at[m],
            recv_sem=xs_recv.at[m],
            device_id={"voc": h * NX + xt},
            device_id_type=MESH,
        )

    def gather(m, k):
        xt = lax.rem(x + k, NX)
        return pltpu.make_async_remote_copy(
            src_ref=total.at[m, x],
            dst_ref=total.at[m, x],
            send_sem=xg_send.at[m],
            recv_sem=xg_recv.at[m],
            device_id={"voc": h * NX + xt},
            device_id_type=MESH,
        )

    def cross(m):
        return pltpu.make_async_remote_copy(
            src_ref=half.at[m],
            dst_ref=half_in.at[m],
            send_sem=y_send.at[m],
            recv_sem=y_recv.at[m],
            device_id=across,
            device_id_type=MESH,
        )

    def others(ref, sem):
        few = ref.at[pl.ds(0, NX - 1)]
        pltpu.make_async_copy(few, few, sem).wait()

    def block(m, j):
        return grad[m, :, pl.ds(j * NZ, NZ)].reshape(rows, cg)

    for m in range(mb):
        pltpu.make_async_copy(grad.at[m, core], grad.at[m, core], two_recv.at[m]).wait()
        forward(m).start()
        forward(m).wait_recv()

        part[m] = jnp.zeros((rows, width), F32)

        @pl.loop(0, NY)
        def _(j):
            at = pl.multiple_of(j * cg, cg)
            part[m] += jnp.dot(block(m, j), weight_t[pl.ds(at, cg), :], preferred_element_type=F32)

        part_b[m] = part[m].astype(BF16).reshape(NX, quarter, width)
        for k in range(1, NX):
            scatter(m, k).start()
        if m == mb - 1:
            for j in range(NY):
                cols = pl.ds(j * cg, cg)
                out = jnp.dot(ordered_t[0], block(0, j), preferred_element_type=F32)
                for n in range(1, mb):
                    out += jnp.dot(ordered_t[n], block(n, j), preferred_element_type=F32)
                head_out[:, cols] = out.astype(BF16)
                pltpu.make_async_copy(head_out.at[:, cols], head_hbm.at[:, cols], out_sem.at[0]).start()

        others(xin.at[m], xs_recv.at[m])
        acc = part[m, pl.ds(pl.multiple_of(x * quarter, quarter), quarter), :]
        for k in range(1, NX):
            acc += xin[m, lax.rem(x + k, NX)].astype(F32)
        half[m] = acc.astype(BF16)
        if NH > 1:
            cross(m).start()
            cross(m).wait_recv()
            total[m, x] = (half[m].astype(F32) + half_in[m].astype(F32)).astype(BF16)
        else:
            total[m, x] = half[m]
        for k in range(1, NX):
            gather(m, k).start()
        others(total.at[m], xg_recv.at[m])
        state_out[m] = lax.dot_general(
            onehot[m],
            total[m].reshape(rows, width),
            (((0,), (0,)), ((), ())),
            preferred_element_type=F32,
        ).astype(BF16)
        pltpu.make_async_copy(state_out.at[m], state_hbm.at[m], out_sem.at[1]).start()

    most = logits.at[0, pl.ds(0, count - 1)]
    for m in range(mb):
        for u in range(2):
            pair_copy(m, u).wait_send()
        pltpu.make_async_copy(most, most, one_send.at[m]).wait()
        pltpu.make_async_copy(most, most, two_send.at[m]).wait()
        forward(m).wait_send()
        others(part_b.at[m], xs_send.at[m])
        others(total.at[m], xg_send.at[m])
        if NH > 1:
            cross(m).wait_send()
    pltpu.make_async_copy(head_out, head_hbm, out_sem.at[0]).wait()
    pltpu.make_async_copy(state_out, state_hbm, out_sem.at[1]).wait()


def build(mesh, dims):
    NZ, NY, NX, NH = dims

    def body(states, head_weight, pair_order, row_example):
        mb, rows, width = states.shape
        vocab = head_weight.shape[1]
        count = NZ * NY
        side = rows // 2
        rg, cg = side // NZ, vocab // NY
        quarter = rows // NX
        vm = pltpu.VMEM
        dma = pltpu.SemaphoreType.DMA
        hbm = pl.BlockSpec(memory_space=pl.ANY)
        return pl.pallas_call(
            functools.partial(kernel, dims),
            out_shape=(
                jax.ShapeDtypeStruct(states.shape, BF16),
                jax.ShapeDtypeStruct(head_weight.shape, BF16),
            ),
            in_specs=[pl.BlockSpec(memory_space=pltpu.SMEM), hbm, hbm, hbm],
            out_specs=(hbm, hbm),
            scratch_shapes=[
                vm((width, vocab), BF16),
                vm((vocab, width), BF16),
                vm((mb, rows, width), BF16),
                vm(row_example.shape, jnp.int32),
                vm((mb, rows, rows), BF16),
                vm((mb, rows, width), BF16),
                vm((mb, width, rows), BF16),
                vm((mb, 2, side // 2, vocab), F32),
                vm((mb, 2, side // 2, vocab), F32),
                vm((mb, 2, side // 2, vocab), F32),
                vm((mb, count, rg, cg), BF16),
                vm((count, rg, cg), BF16),
                vm((count, rg, cg), BF16),
                vm((mb, count, rg, cg), BF16),
                vm((mb, 2, count, rg, cg), BF16),
                vm((mb, rows, width), F32),
                vm((mb, NX, quarter, width), BF16),
                vm((mb, NX, quarter, width), BF16),
                vm((mb, quarter, width), BF16),
                vm((mb, quarter, width), BF16),
                vm((mb, NX, quarter, width), BF16),
                vm((mb, rows, width), BF16),
                vm((width, vocab), BF16),
                pltpu.SMEM((mb, count), jnp.int32),
                dma((3,)),
                dma((2,)),
                dma((mb, 2)),
                dma((mb, 2)),
            ]
            + [dma((mb,))] * 12,
            compiler_params=pltpu.CompilerParams(
                collective_id=0, has_side_effects=True, vmem_limit_bytes=56 * 1024 * 1024
            ),
        )(pair_order, states, head_weight, row_example)

    return jax.shard_map(
        body,
        mesh=mesh,
        in_specs=(P(None, None, "rep"), P("rep", "voc"), P(), P()),
        out_specs=(P(None, None, "rep"), P("rep", "voc")),
        check_vma=False,
    )


def solution(mesh):
    return build(mesh, (8, 4, 4, 2))
```

```python
import functools

import jax
import jax.numpy as jnp
from jax import lax
from jax.experimental import pallas as pl
from jax.experimental.pallas import tpu as pltpu
from jax.sharding import PartitionSpec as P

MESH = pl.DeviceIdType.MESH
SCALE = 0.0625
CUTS = 2
TALL = 16
F32, BF16 = jnp.float32, jnp.bfloat16
scope = jax.named_scope


def kernel(
    dims,
    order_hbm,
    states_hbm,
    weight_hbm,
    example_hbm,
    state_hbm,
    head_hbm,
    pair_order,
    weight,
    weight_t,
    states,
    examples,
    onehot,
    ordered,
    ordered_t,
    mine,
    sent,
    got,
    logits,
    pools,
    spread,
    grad,
    part,
    part_b,
    xin,
    half,
    half_in,
    total,
    state_out,
    head_out,
    partner,
    in_sem,
    out_sem,
    pair_send,
    pair_recv,
    one_send,
    one_recv,
    two_send,
    two_recv,
    fwd_send,
    fwd_recv,
    xs_send,
    xs_recv,
    y_send,
    y_recv,
    xg_send,
    xg_recv,
):
    NZ, NY, NX, NH = dims
    mb, rows, width = states.shape
    vocab = weight.shape[1]
    count = NZ * NY
    chunks = CUTS * mb
    crows = rows // CUTS
    srows = crows // 2
    rows_n = srows // TALL
    cols_n = count // rows_n
    cg = vocab // cols_n
    quarter = crows // NX

    rep, voc = lax.axis_index("rep"), lax.axis_index("voc")
    core = lax.rem(rep, 2)
    rid = rep // 2
    z, y = rid // NY, lax.rem(rid, NY)
    h, x = voc // NX, lax.rem(voc, NX)
    pair = {"rep": rid * 2 + 1 - core}
    across = {"voc": (NH - 1 - h) * NX + x}

    loads = [
        pltpu.make_async_copy(example_hbm, examples, in_sem.at[0]),
        pltpu.make_async_copy(states_hbm, states, in_sem.at[1]),
        pltpu.make_async_copy(weight_hbm, weight, in_sem.at[2]),
        pltpu.make_async_copy(order_hbm, pair_order, in_sem.at[3]),
    ]
    barrier = pltpu.get_barrier_semaphore()

    def greet():
        for k in range(1, count):
            pl.semaphore_signal(
                barrier,
                inc=1,
                device_id={"rep": lax.rem(rid + k, count) * 2 + core},
                device_id_type=MESH,
            )

        pl.semaphore_signal(barrier, inc=1, device_id=pair, device_id_type=MESH)
        for k in range(1, NX):
            pl.semaphore_signal(
                barrier, inc=1, device_id={"voc": h * NX + lax.rem(x + k, NX)}, device_id_type=MESH
            )
        pl.semaphore_signal(barrier, inc=1, device_id=across, device_id_type=MESH)

    def order():
        ids = lax.broadcasted_iota(jnp.int32, (rows, rows), 0)
        for m in range(mb):
            row = examples[m, pl.ds(rid, 1), :]
            onehot[m] = (ids == row).astype(BF16)
            ordered[m] = jnp.dot(onehot[m], states[m], preferred_element_type=F32).astype(BF16)

    def partials(side, target):
        left = []
        for q in range(chunks):
            at = pl.multiple_of((q % CUTS) * crows + side * srows, srows)
            left.append(ordered[q // CUTS, pl.ds(at, srows), :])
        left = jnp.concatenate(left, axis=0)

        @pl.loop(0, 4)
        def _(j):
            cols = pl.ds(pl.multiple_of(j * (vocab // 4), vocab // 4), vocab // 4)
            out = jnp.dot(left, weight[:, cols], preferred_element_type=F32)
            for q in range(chunks):
                target[q, :, cols] = out[q * srows : (q + 1) * srows]

    def pair_copy(q):
        return pltpu.make_async_remote_copy(
            src_ref=sent.at[q],
            dst_ref=got.at[q],
            send_sem=pair_send.at[q],
            recv_sem=pair_recv.at[q],
            device_id=pair,
            device_id_type=MESH,
        )

    def send(r, src, dst, send_sem, recv_sem):
        pltpu.make_async_remote_copy(
            src_ref=src,
            dst_ref=dst,
            send_sem=send_sem,
            recv_sem=recv_sem,
            device_id={"rep": r * 2 + core},
            device_id_type=MESH,
        ).start()

    def settle(q):
        @pl.loop(0, 4)
        def _(j):
            cols = pl.ds(pl.multiple_of(j * (vocab // 4), vocab // 4), vocab // 4)
            both = (mine[q, :, cols] + got[q, :, cols]).astype(BF16)
            for i in range(cols_n // 4):
                piece = both[:, i * cg : (i + 1) * cg].reshape(rows_n, TALL, cg)
                logits[q, pl.ds((j * (cols_n // 4) + i) * rows_n, rows_n)] = piece

        @pl.loop(1, count)
        def _(k):
            r = lax.rem(rid + k, count)
            send(r, logits.at[q, r], pools[q].at[rid], one_send.at[q], one_recv.at[q])

        pltpu.make_async_copy(logits.at[q, rid], pools[q].at[rid], one_recv.at[q]).start()

    def tables():
        loads[3].wait()
        for m in range(mb):

            @pl.loop(0, count)
            def _(r):
                found = jnp.int32(0)
                for k in range(count):
                    found += jnp.where(pair_order[m, k] == r, pair_order[m, (k + 1) % count], 0)
                partner[m, r] = found

    def turn():
        for m in range(mb):
            ordered_t[:, m * rows : (m + 1) * rows] = ordered[m].T

        @pl.loop(0, 4)
        def _(j):
            at = pl.multiple_of(j * (vocab // 4), vocab // 4)
            weight_t[pl.ds(at, vocab // 4), :] = weight[:, pl.ds(at, vocab // 4)].T

    def compare(q):
        pool, batch = pools[q], 8

        def differ(r):
            own, other = pool[r], pool[partner[q // CUTS, r]]
            spread[q, r] = (SCALE * (own.astype(F32) - other.astype(F32))).astype(BF16)

        @pl.loop(0, count // batch)
        def _(b):
            for i in range(batch):
                differ(lax.rem(rid + 1 + b * batch + i, count))
            for i in range(batch - 1):
                r = lax.rem(rid + 1 + b * batch + i, count)
                send(r, spread.at[q, r], grad.at[q, core, rid], two_send.at[q], two_recv.at[q])

            @pl.when(b < count // batch - 1)
            def _():
                r = lax.rem(rid + 1 + b * batch + batch - 1, count)
                send(r, spread.at[q, r], grad.at[q, core, rid], two_send.at[q], two_recv.at[q])

        pltpu.make_async_copy(spread.at[q, rid], grad.at[q, core, rid], two_recv.at[q]).start()

    def await_ref(ref, sem):
        pltpu.make_async_copy(ref, ref, sem).wait()

    def forward(q):
        return pltpu.make_async_remote_copy(
            src_ref=grad.at[q, core],
            dst_ref=grad.at[q, core],
            send_sem=fwd_send.at[q],
            recv_sem=fwd_recv.at[q],
            device_id=pair,
            device_id_type=MESH,
        )

    def scatter(q, k):
        xt = lax.rem(x + k, NX)
        return pltpu.make_async_remote_copy(
            src_ref=part_b.at[q, xt],
            dst_ref=xin.at[q, x],
            send_sem=xs_send.at[q],
            recv_sem=xs_recv.at[q],
            device_id={"voc": h * NX + xt},
            device_id_type=MESH,
        )

    def gather(q, k):
        xt = lax.rem(x + k, NX)
        return pltpu.make_async_remote_copy(
            src_ref=total.at[q, x],
            dst_ref=total.at[q, x],
            send_sem=xg_send.at[q],
            recv_sem=xg_recv.at[q],
            device_id={"voc": h * NX + xt},
            device_id_type=MESH,
        )

    def cross(q):
        return pltpu.make_async_remote_copy(
            src_ref=half.at[q],
            dst_ref=half_in.at[q],
            send_sem=y_send.at[q],
            recv_sem=y_recv.at[q],
            device_id=across,
            device_id_type=MESH,
        )

    def others(ref, sem):
        few = ref.at[pl.ds(0, NX - 1)]
        pltpu.make_async_copy(few, few, sem).wait()

    def block(q, j):
        return grad[q, :, pl.ds(j * rows_n, rows_n)].reshape(crows, cg)

    def state_part(q):
        lhs = jnp.concatenate([block(q, j) for j in range(cols_n)], axis=1)
        out = jnp.dot(lhs, weight_t[...], preferred_element_type=F32)
        part[q] = out
        part_b[q] = out.astype(BF16).reshape(NX, quarter, width)

    def head():
        per = cols_n // 8
        wide = vocab // 8
        for j in range(8):
            cols = pl.ds(j * wide, wide)
            right = jnp.concatenate(
                [
                    jnp.concatenate([block(q, j * per + i) for i in range(per)], axis=1)
                    for q in range(chunks)
                ],
                axis=0,
            )
            out = jnp.dot(ordered_t[...], right, preferred_element_type=F32)
            head_out[:, cols] = out.astype(BF16)
            pltpu.make_async_copy(head_out.at[:, cols], head_hbm.at[:, cols], out_sem.at[0]).start()

    def sum_x(q):
        acc = part[q, pl.ds(pl.multiple_of(x * quarter, quarter), quarter), :]
        for k in range(1, NX):
            acc += xin[q, lax.rem(x + k, NX)].astype(F32)
        half[q] = acc.astype(BF16)

    def sum_h(q):
        total[q, x] = (half[q].astype(F32) + half_in[q].astype(F32)).astype(BF16)

    def restore(m):
        state_out[m] = lax.dot_general(
            onehot[m],
            total[CUTS * m : CUTS * m + CUTS].reshape(rows, width),
            (((0,), (0,)), ((), ())),
            preferred_element_type=F32,
        ).astype(BF16)
        pltpu.make_async_copy(state_out.at[m], state_hbm.at[m], out_sem.at[1]).start()

    def x_stage(q):
        with scope(f"xs_wait{q}"):
            others(xin.at[q], xs_recv.at[q])
        sum_x(q)
        cross(q).start()

    def y_stage(q):
        with scope(f"y_wait{q}"):
            cross(q).wait_recv()
        sum_h(q)
        for k in range(1, NX):
            gather(q, k).start()

    def done(q):
        with scope(f"xg_wait{q}"):
            others(total.at[q], xg_recv.at[q])

    for load in loads:
        load.start()
    with scope("greet"):
        greet()
    with scope("load"):
        loads[0].wait()
        loads[1].wait()
    with scope("order"):
        order()
    with scope("loadw"):
        loads[2].wait()
    with scope("partial0"):
        partials(1 - core, sent)
    with scope("barrier"):
        pl.semaphore_wait(barrier, count - 1 + 1 + NX - 1 + 1)
    for q in range(chunks):
        pair_copy(q).start()
    with scope("partial1"):
        partials(core, mine)
    for q in range(chunks):
        with scope(f"pairwait{q}"):
            pair_copy(q).wait_recv()
        with scope(f"settle{q}"):
            settle(q)
    with scope("tables"):
        tables()
    with scope("turn"):
        turn()
    for q in range(chunks):
        with scope(f"wait1_{q}"):
            await_ref(pools[q], one_recv.at[q])
        with scope(f"compare{q}"):
            compare(q)
    for q in range(chunks + 3):
        last = q == chunks - 1
        if q < chunks:
            with scope(f"wait2_{q}"):
                await_ref(grad.at[q, core], two_recv.at[q])
            with scope(f"forward{q}"):
                forward(q).start()
                forward(q).wait_recv()
            with scope(f"state_part{q}"):
                state_part(q)
            for k in range(1, NX):
                scatter(q, k).start()
            if last:
                x_stage(q - 1)
                y_stage(q - 2)
                with scope("head"):
                    head()
        if q == chunks:
            x_stage(q - 1)
            y_stage(q - 2)
        elif not last:
            if 0 <= q - 1 < chunks:
                x_stage(q - 1)
            if 0 <= q - 2 < chunks:
                y_stage(q - 2)
        if 0 <= q - 3 < chunks:
            done(q - 3)
            if q - 3 < chunks - 1 and (q - 3) % CUTS == CUTS - 1:
                with scope(f"restore{q-3}"):
                    restore((q - 3) // CUTS)
    with scope("restore"):
        restore(mb - 1)

    with scope("drain"):
        most = logits.at[0, pl.ds(0, count - 1)]
        for q in range(chunks):
            pair_copy(q).wait_send()
            await_ref(most, one_send.at[q])
            await_ref(most, two_send.at[q])
            forward(q).wait_send()
            others(part_b.at[q], xs_send.at[q])
            others(total.at[q], xg_send.at[q])
            cross(q).wait_send()
        pltpu.make_async_copy(head_out, head_hbm, out_sem.at[0]).wait()
        pltpu.make_async_copy(state_out, state_hbm, out_sem.at[1]).wait()


def finish(state_in, head_in, state_out, head_out, state, head, in_sem, out_sem):
    pieces = 4
    step = head.shape[0] // pieces
    moves = []
    for p in range(pieces):
        at = pl.ds(p * step, step)
        moves.append((head_in.at[at], head.at[at], head_out.at[at]))
    for m in range(state.shape[0]):
        moves.append((state_in.at[m], state.at[m], state_out.at[m]))
    ins = [pltpu.make_async_copy(a, b, in_sem.at[i]) for i, (a, b, _) in enumerate(moves)]
    outs = [pltpu.make_async_copy(b, c, out_sem.at[i]) for i, (_, b, c) in enumerate(moves)]
    for copy in ins:
        copy.start()
    for copy_in, copy_out in zip(ins, outs):
        copy_in.wait()
        copy_out.start()
    for copy in outs:
        copy.wait()


def build(mesh, dims):
    NZ, NY, NX, NH = dims

    def body(states, head_weight, pair_order, row_example):
        mb, rows, width = states.shape
        vocab = head_weight.shape[1]
        count = NZ * NY
        chunks = CUTS * mb
        crows = rows // CUTS
        srows = crows // 2
        slot = (count, TALL, vocab * srows // (count * TALL))
        quarter = crows // NX
        vm = pltpu.VMEM
        dma = pltpu.SemaphoreType.DMA
        hbm = pl.BlockSpec(memory_space=pl.ANY)
        shapes = (
            jax.ShapeDtypeStruct(states.shape, BF16),
            jax.ShapeDtypeStruct(head_weight.shape, BF16),
        )
        made = pl.pallas_call(
            functools.partial(kernel, dims),
            out_shape=shapes,
            in_specs=[hbm, hbm, hbm, hbm],
            out_specs=(hbm, hbm),
            scratch_shapes=[
                pltpu.SMEM((mb, count), jnp.int32),
                vm((width, vocab), BF16),
                vm((vocab, width), BF16),
                vm((mb, rows, width), BF16),
                vm(row_example.shape, jnp.int32),
                vm((mb, rows, rows), BF16),
                vm((mb, rows, width), BF16),
                vm((width, mb * rows), BF16),
                vm((chunks, srows, vocab), F32),
                vm((chunks, srows, vocab), F32),
                vm((chunks, srows, vocab), F32),
                vm((chunks, *slot), BF16),
            ]
            + [[vm(slot, BF16)] * chunks]
            + [
                vm((chunks, *slot), BF16),
                vm((chunks, 2, *slot), BF16),
                vm((chunks, crows, width), F32),
                vm((chunks, NX, quarter, width), BF16),
                vm((chunks, NX, quarter, width), BF16),
                vm((chunks, quarter, width), BF16),
                vm((chunks, quarter, width), BF16),
                vm((chunks, NX, quarter, width), BF16),
                vm((mb, rows, width), BF16),
                vm((width, vocab), BF16),
                pltpu.SMEM((mb, count), jnp.int32),
                dma((4,)),
                dma((2,)),
            ]
            + [dma((chunks,))] * 14,
            compiler_params=pltpu.CompilerParams(
                collective_id=0, has_side_effects=True, vmem_limit_bytes=60 * 1024 * 1024
            ),
        )(pair_order, states, head_weight, row_example)
        pieces = 4 + mb
        return pl.pallas_call(
            finish,
            out_shape=shapes,
            in_specs=[hbm, hbm],
            out_specs=(hbm, hbm),
            scratch_shapes=[
                vm(states.shape, BF16),
                vm(head_weight.shape, BF16),
                dma((pieces,)),
                dma((pieces,)),
            ],
            compiler_params=pltpu.CompilerParams(vmem_limit_bytes=60 * 1024 * 1024),
        )(*made)

    return jax.shard_map(
        body,
        mesh=mesh,
        in_specs=(P(None, None, "rep"), P("rep", "voc"), P(), P()),
        out_specs=(P(None, None, "rep"), P("rep", "voc")),
        check_vma=False,
    )


def solution(mesh):
    return build(mesh, (8, 4, 4, 2))
```

```python
import functools

import jax
import jax.numpy as jnp
from jax import lax
from jax.experimental import pallas as pl
from jax.experimental.pallas import tpu as pltpu
from jax.sharding import PartitionSpec as P

MESH = pl.DeviceIdType.MESH
SCALE = 0.0625
PLAN = ((0, 64), (0, 64), (1, 64), (1, 64))
TALL = 16
F32, BF16 = jnp.float32, jnp.bfloat16
scope = jax.named_scope


def kernel(
    dims,
    order_hbm,
    states_hbm,
    weight_hbm,
    example_hbm,
    state_hbm,
    head_hbm,
    pair_order,
    weight,
    weight_t,
    states,
    examples,
    onehot,
    ordered,
    ordered_t,
    mine,
    sent,
    got,
    logits,
    pools,
    spread,
    grad,
    part,
    part_b,
    xin,
    half,
    half_in,
    final,
    total,
    state_out,
    head_out,
    partner,
    in_sem,
    out_sem,
    pair_send,
    pair_recv,
    one_send,
    one_recv,
    two_send,
    two_recv,
    fwd_send,
    fwd_recv,
    turn_sem,
    xs_send,
    xs_recv,
    y_send,
    y_recv,
    xg_send,
    xg_recv,
):
    NZ, NY, NX, NH = dims
    mb, rows, width = states.shape
    vocab = weight.shape[1]
    count = NZ * NY
    chunks = len(PLAN)
    micro = [m for m, _ in PLAN]
    srows = [n for _, n in PLAN]
    first = [2 * sum(n for p, n in PLAN[:q] if p == micro[q]) for q in range(chunks)]
    base = [sum(srows[:q]) for q in range(chunks)]
    rows_n = [n // TALL for n in srows]
    cols_n = [count // n for n in rows_n]
    cgs = [vocab // n for n in cols_n]
    quarter = [n // NX for n in srows]

    rep, voc = lax.axis_index("rep"), lax.axis_index("voc")
    core = lax.rem(rep, 2)
    rid = rep // 2
    z, y = rid // NY, lax.rem(rid, NY)
    h, x = voc // NX, lax.rem(voc, NX)
    pair = {"rep": rid * 2 + 1 - core}
    across = {"voc": (NH - 1 - h) * NX + x}

    def along(k, other):
        there = 1 - core if other else core
        return {"rep": rid * 2 + there, "voc": h * NX + lax.rem(x + k, NX)}


    loads = [
        pltpu.make_async_copy(example_hbm, examples, in_sem.at[0]),
        pltpu.make_async_copy(states_hbm, states, in_sem.at[1]),
        pltpu.make_async_copy(weight_hbm, weight, in_sem.at[2]),
        pltpu.make_async_copy(order_hbm, pair_order, in_sem.at[3]),
    ]
    barrier = pltpu.get_barrier_semaphore()

    def greet():
        for k in sorted(range(1, count), key=lambda k: -min(k, count - k)):
            pl.semaphore_signal(
                barrier,
                inc=1,
                device_id={"rep": lax.rem(rid + k, count) * 2 + core},
                device_id_type=MESH,
            )

        pl.semaphore_signal(barrier, inc=1, device_id=pair, device_id_type=MESH)
        for k in range(1, NX):
            for other in range(2):
                pl.semaphore_signal(
                    barrier, inc=1, device_id=along(k, other), device_id_type=MESH
                )
        pl.semaphore_signal(barrier, inc=1, device_id=across, device_id_type=MESH)

    def order():
        ids = lax.broadcasted_iota(jnp.int32, (rows, rows), 0)
        for m in range(mb):
            row = examples[m, pl.ds(rid, 1), :]
            onehot[m] = (ids == row).astype(BF16)
            ordered[m] = jnp.dot(onehot[m], states[m], preferred_element_type=F32).astype(BF16)

    def partials(side, target):
        left = []
        for q in range(chunks):
            at = pl.multiple_of(first[q] + side * srows[q], srows[q])
            left.append(ordered[micro[q], pl.ds(at, srows[q]), :])
        left = jnp.concatenate(left, axis=0)

        @pl.loop(0, 4)
        def _(j):
            cols = pl.ds(pl.multiple_of(j * (vocab // 4), vocab // 4), vocab // 4)
            out = jnp.dot(left, weight[:, cols], preferred_element_type=F32)
            target[:, cols] = out

    def pair_copy(q):
        return pltpu.make_async_remote_copy(
            src_ref=sent.at[pl.ds(base[q], srows[q])],
            dst_ref=got.at[pl.ds(base[q], srows[q])],
            send_sem=pair_send.at[q],
            recv_sem=pair_recv.at[q],
            device_id=pair,
            device_id_type=MESH,
        )

    def send(r, src, dst, send_sem, recv_sem):
        pltpu.make_async_remote_copy(
            src_ref=src,
            dst_ref=dst,
            send_sem=send_sem,
            recv_sem=recv_sem,
            device_id={"rep": r * 2 + core},
            device_id_type=MESH,
        ).start()

    def settle(q):
        rn, cg, per = rows_n[q], cgs[q], cols_n[q] // 4
        at = pl.ds(base[q], srows[q])

        @pl.loop(0, 4)
        def _(j):
            cols = pl.ds(pl.multiple_of(j * (vocab // 4), vocab // 4), vocab // 4)
            both = (mine[at, cols] + got[at, cols]).astype(BF16)
            for i in range(per):
                piece = both[:, i * cg : (i + 1) * cg].reshape(rn, TALL, cg)
                logits[q][pl.ds((j * per + i) * rn, rn)] = piece

        @pl.loop(1, count)
        def _(k):
            r = lax.rem(rid + k, count)
            send(r, logits[q].at[r], pools[q].at[rid], one_send.at[q], one_recv.at[q])

        pltpu.make_async_copy(logits[q].at[rid], pools[q].at[rid], one_recv.at[q]).start()

    def tables():
        loads[3].wait()
        for m in range(mb):

            @pl.loop(0, count)
            def _(r):
                found = jnp.int32(0)
                for k in range(count):
                    found += jnp.where(pair_order[m, k] == r, pair_order[m, (k + 1) % count], 0)
                partner[m, r] = found

    def turn():
        for m in range(mb):
            ordered_t[:, m * rows : (m + 1) * rows] = ordered[m].T

        @pl.loop(0, 4)
        def _(j):
            at = pl.multiple_of(j * (vocab // 4), vocab // 4)
            weight_t[core, pl.ds(at, vocab // 4), :] = weight[:, pl.ds(at, vocab // 4)].T

    def compare(q):
        pool, batch = pools[q], 8

        def differ(r):
            own, other = pool[r], pool[partner[micro[q], r]]
            spread[q][r] = (SCALE * (own.astype(F32) - other.astype(F32))).astype(BF16)

        @pl.loop(0, count // batch)
        def _(b):
            for i in range(batch):
                differ(lax.rem(rid + 1 + b * batch + i, count))
            for i in range(batch - 1):
                r = lax.rem(rid + 1 + b * batch + i, count)
                send(r, spread[q].at[r], grad[q].at[core, rid], two_send.at[q], two_recv.at[q])

            @pl.when(b < count // batch - 1)
            def _():
                r = lax.rem(rid + 1 + b * batch + batch - 1, count)
                send(r, spread[q].at[r], grad[q].at[core, rid], two_send.at[q], two_recv.at[q])

        pltpu.make_async_copy(spread[q].at[rid], grad[q].at[core, rid], two_recv.at[q]).start()

    def await_ref(ref, sem):
        pltpu.make_async_copy(ref, ref, sem).wait()

    def forward(q):
        return pltpu.make_async_remote_copy(
            src_ref=grad[q].at[core],
            dst_ref=grad[q].at[core],
            send_sem=fwd_send.at[q],
            recv_sem=fwd_recv.at[q],
            device_id=pair,
            device_id_type=MESH,
        )

    def turned():
        return pltpu.make_async_remote_copy(
            src_ref=weight_t.at[core],
            dst_ref=weight_t.at[core],
            send_sem=turn_sem.at[0],
            recv_sem=turn_sem.at[1],
            device_id=pair,
            device_id_type=MESH,
        )

    def scatter(q, k):
        return pltpu.make_async_remote_copy(
            src_ref=part_b[q].at[lax.rem(x + k, NX)],
            dst_ref=xin[q].at[x],
            send_sem=xs_send.at[q],
            recv_sem=xs_recv.at[q],
            device_id=along(k, 0),
            device_id_type=MESH,
        )

    def gather(q):
        dst = total[q].at[core * NX + x]
        for k in sorted(range(NX), key=lambda k: -min(k, NX - k)):
            for other in range(2):
                if k or other:
                    pltpu.make_async_remote_copy(
                        src_ref=final[q].at[1 - core if other else core],
                        dst_ref=dst,
                        send_sem=xg_send.at[q],
                        recv_sem=xg_recv.at[q],
                        device_id=along(k, other),
                        device_id_type=MESH,
                    ).start()
        total[q][core * NX + x] = final[q][core]

    def cross(q):
        return pltpu.make_async_remote_copy(
            src_ref=half[q],
            dst_ref=half_in[q],
            send_sem=y_send.at[q],
            recv_sem=y_recv.at[q],
            device_id=across,
            device_id_type=MESH,
        )

    def others(ref, sem):
        few = ref.at[pl.ds(0, ref.shape[0] - 1)]
        pltpu.make_async_copy(few, few, sem).wait()

    def state_part(q):
        lhs = jnp.concatenate(
            [
                grad[q][core, pl.ds(j * rows_n[q], rows_n[q])].reshape(srows[q], cgs[q])
                for j in range(cols_n[q])
            ],
            axis=1,
        )
        for w in range(2):
            out = jnp.dot(lhs, weight_t[w], preferred_element_type=F32)
            part[q][w] = out
            part_b[q][:, w] = out.reshape(NX, quarter[q], width).astype(BF16)

    def head():
        wide = vocab // 8
        for j in range(8):
            cols = pl.ds(j * wide, wide)
            right = []
            for q in range(chunks):
                per, rn = cols_n[q] // 8, rows_n[q]
                right.append(
                    jnp.concatenate(
                        [
                            grad[q][:, pl.ds((j * per + i) * rn, rn)].reshape(2 * srows[q], cgs[q])
                            for i in range(per)
                        ],
                        axis=1,
                    )
                )
            right = jnp.concatenate(right, axis=0)
            out = jnp.dot(ordered_t[...], right, preferred_element_type=F32)
            head_out[:, cols] = out.astype(BF16)
            pltpu.make_async_copy(head_out.at[:, cols], head_hbm.at[:, cols], out_sem.at[0]).start()

    def sum_x(q):
        acc = part[q][:, pl.ds(pl.multiple_of(x * quarter[q], quarter[q]), quarter[q]), :]
        for k in range(1, NX):
            acc += xin[q][lax.rem(x + k, NX)].astype(F32)
        half[q][...] = acc.astype(BF16)

    def sum_h(q):
        final[q][...] = (half[q][...].astype(F32) + half_in[q][...].astype(F32)).astype(BF16)

    def restore(m):
        rows_of = [
            total[q][...].astype(F32).reshape(2 * srows[q], width).astype(BF16)
            for q in range(chunks)
            if micro[q] == m
        ]
        state_out[m] = lax.dot_general(
            onehot[m],
            jnp.concatenate(rows_of, axis=0),
            (((0,), (0,)), ((), ())),
            preferred_element_type=F32,
        ).astype(BF16)
        pltpu.make_async_copy(state_out.at[m], state_hbm.at[m], out_sem.at[1]).start()

    def x_stage(q):
        with scope(f"xs_wait{q}"):
            others(xin[q], xs_recv.at[q])
        sum_x(q)
        cross(q).start()

    def y_stage(q):
        with scope(f"y_wait{q}"):
            cross(q).wait_recv()
        sum_h(q)
        gather(q)

    def done(q):
        with scope(f"xg_wait{q}"):
            others(total[q], xg_recv.at[q])

    for load in loads:
        load.start()
    with scope("greet"):
        greet()
    with scope("load"):
        loads[0].wait()
        loads[1].wait()
    with scope("order"):
        order()
    with scope("loadw"):
        loads[2].wait()
    with scope("partial0"):
        partials(1 - core, sent)
    with scope("partial1"):
        partials(core, mine)
    with scope("barrier"):
        pl.semaphore_wait(barrier, count - 1 + 1 + 2 * (NX - 1) + 1)
    for q in range(chunks):
        pair_copy(q).start()
    for q in range(chunks):
        with scope(f"pairwait{q}"):
            pair_copy(q).wait_recv()
        with scope(f"settle{q}"):
            settle(q)
    with scope("turn"):
        turn()
    turned().start()
    with scope("tables"):
        tables()
    for q in range(chunks):
        with scope(f"wait1_{q}"):
            await_ref(pools[q], one_recv.at[q])
        with scope(f"compare{q}"):
            compare(q)
    turned().wait_recv()
    for q in range(chunks):
        with scope(f"wait2_{q}"):
            await_ref(grad[q].at[core], two_recv.at[q])
        forward(q).start()
        with scope(f"state_part{q}"):
            state_part(q)
        for k in sorted(range(1, NX), key=lambda k: -min(k, NX - k)):
            scatter(q, k).start()
        if q > 0:
            x_stage(q - 1)
        if q > 2:
            y_stage(q - 3)
    x_stage(chunks - 1)
    y_stage(chunks - 3)
    with scope("fwd_wait"):
        for q in range(chunks):
            forward(q).wait_recv()
    with scope("head"):
        head()
    y_stage(chunks - 2)
    y_stage(chunks - 1)
    for m in range(mb):
        for q in range(chunks):
            if micro[q] == m:
                done(q)
        with scope(f"restore{m}"):
            restore(m)

    with scope("drain"):
        turned().wait_send()
        for q in range(chunks):
            pair_copy(q).wait_send()
            others(logits[q], one_send.at[q])
            others(spread[q], two_send.at[q])
            forward(q).wait_send()
            others(part_b[q], xs_send.at[q])
            others(total[q], xg_send.at[q])
            cross(q).wait_send()
        pltpu.make_async_copy(head_out, head_hbm, out_sem.at[0]).wait()
        pltpu.make_async_copy(state_out, state_hbm, out_sem.at[1]).wait()


def finish(state_in, head_in, state_out, head_out, state, head, in_sem, out_sem):
    pieces = 4
    step = head.shape[0] // pieces
    moves = []
    for p in range(pieces):
        at = pl.ds(p * step, step)
        moves.append((head_in.at[at], head.at[at], head_out.at[at]))
    for m in range(state.shape[0]):
        moves.append((state_in.at[m], state.at[m], state_out.at[m]))
    ins = [pltpu.make_async_copy(a, b, in_sem.at[i]) for i, (a, b, _) in enumerate(moves)]
    outs = [pltpu.make_async_copy(b, c, out_sem.at[i]) for i, (_, b, c) in enumerate(moves)]
    for copy in ins:
        copy.start()
    for copy_in, copy_out in zip(ins, outs):
        copy_in.wait()
        copy_out.start()
    for copy in outs:
        copy.wait()


def build(mesh, dims):
    NZ, NY, NX, NH = dims

    def body(states, head_weight, pair_order, row_example):
        mb, rows, width = states.shape
        vocab = head_weight.shape[1]
        count = NZ * NY
        chunks = len(PLAN)
        srows = [n for _, n in PLAN]
        slots = [(count, TALL, vocab * n // (count * TALL)) for n in srows]
        quarter = [n // NX for n in srows]
        vm = pltpu.VMEM
        dma = pltpu.SemaphoreType.DMA
        hbm = pl.BlockSpec(memory_space=pl.ANY)
        shapes = (
            jax.ShapeDtypeStruct(states.shape, BF16),
            jax.ShapeDtypeStruct(head_weight.shape, BF16),
        )
        made = pl.pallas_call(
            functools.partial(kernel, dims),
            out_shape=shapes,
            in_specs=[hbm, hbm, hbm, hbm],
            out_specs=(hbm, hbm),
            scratch_shapes=[
                pltpu.SMEM((mb, count), jnp.int32),
                vm((width, vocab), BF16),
                vm((2, vocab, width), BF16),
                vm((mb, rows, width), BF16),
                vm(row_example.shape, jnp.int32),
                vm((mb, rows, rows), BF16),
                vm((mb, rows, width), BF16),
                vm((width, mb * rows), BF16),
                vm((sum(srows), vocab), F32),
                vm((sum(srows), vocab), F32),
                vm((sum(srows), vocab), F32),
                [vm(slot, BF16) for slot in slots],
                [vm(slot, BF16) for slot in slots],
                [vm(slot, BF16) for slot in slots],
                [vm((2, *slot), BF16) for slot in slots],
                [vm((2, n, width), F32) for n in srows],
                [vm((NX, 2, n, width), BF16) for n in quarter],
                [vm((NX, 2, n, width), BF16) for n in quarter],
                [vm((2, n, width), BF16) for n in quarter],
                [vm((2, n, width), BF16) for n in quarter],
                [vm((2, n, width), BF16) for n in quarter],
                [vm((2 * NX, n, width), BF16) for n in quarter],
                vm((mb, rows, width), BF16),
                vm((width, vocab), BF16),
                pltpu.SMEM((mb, count), jnp.int32),
                dma((4,)),
                dma((2,)),
            ]
            + [dma((chunks,))] * 8
            + [dma((2,))]
            + [dma((chunks,))] * 6,
            compiler_params=pltpu.CompilerParams(
                collective_id=0, has_side_effects=True, vmem_limit_bytes=60 * 1024 * 1024
            ),
        )(pair_order, states, head_weight, row_example)
        pieces = 4 + mb
        return pl.pallas_call(
            finish,
            out_shape=shapes,
            in_specs=[hbm, hbm],
            out_specs=(hbm, hbm),
            scratch_shapes=[
                vm(states.shape, BF16),
                vm(head_weight.shape, BF16),
                dma((pieces,)),
                dma((pieces,)),
            ],
            compiler_params=pltpu.CompilerParams(vmem_limit_bytes=60 * 1024 * 1024),
        )(*made)

    return jax.shard_map(
        body,
        mesh=mesh,
        in_specs=(P(None, None, "rep"), P("rep", "voc"), P(), P()),
        out_specs=(P(None, None, "rep"), P("rep", "voc")),
        check_vma=False,
    )


def solution(mesh):
    return build(mesh, (8, 4, 4, 2))
```

```python
import functools

import jax
import jax.numpy as jnp
from jax import lax
from jax.experimental import pallas as pl
from jax.experimental.pallas import tpu as pltpu
from jax.sharding import PartitionSpec as P

MESH = pl.DeviceIdType.MESH
SCALE = 0.0625
GROUPS = ((0, (32, 32)), (0, (64,)), (1, (64,)), (1, (64,)))
PLAN = [(g, sum(ns[:i]), n) for g, (_, ns) in enumerate(GROUPS) for i, n in enumerate(ns)]
TALL = 16
F32, BF16 = jnp.float32, jnp.bfloat16
scope = jax.named_scope


def kernel(
    dims,
    order_hbm,
    states_hbm,
    weight_hbm,
    example_hbm,
    state_hbm,
    head_hbm,
    pair_order,
    weight,
    weight_t,
    states,
    examples,
    onehot,
    ordered,
    ordered_t,
    mine,
    sent,
    got,
    logits,
    pools,
    spread,
    grad,
    part,
    part_b,
    xin,
    half,
    half_in,
    final,
    total,
    state_out,
    head_out,
    partner,
    in_sem,
    out_sem,
    pair_send,
    pair_recv,
    one_send,
    one_recv,
    two_send,
    two_recv,
    fwd_send,
    fwd_recv,
    turn_sem,
    xs_send,
    xs_recv,
    y_send,
    y_recv,
    xg_send,
    xg_recv,
):
    NZ, NY, NX, NH = dims
    mb, rows, width = states.shape
    vocab = weight.shape[1]
    count = NZ * NY
    chunks = len(PLAN)
    groups = len(GROUPS)
    micro = [m for m, _ in GROUPS]
    gs = [sum(ns) for _, ns in GROUPS]
    first = [2 * sum(n for p, n in zip(micro[:g], gs) if p == micro[g]) for g in range(groups)]
    of = [[q for q in range(chunks) if PLAN[q][0] == g] for g in range(groups)]
    srows = [n for _, _, n in PLAN]
    base = [sum(srows[:q]) for q in range(chunks)]
    rows_n = [n // TALL for n in srows]
    cols_n = [count // n for n in rows_n]
    cgs = [vocab // n for n in cols_n]
    quarter = [n // NX for n in gs]

    rep, voc = lax.axis_index("rep"), lax.axis_index("voc")
    core = lax.rem(rep, 2)
    rid = rep // 2
    z, y = rid // NY, lax.rem(rid, NY)
    h, x = voc // NX, lax.rem(voc, NX)
    pair = {"rep": rid * 2 + 1 - core}
    across = {"voc": (NH - 1 - h) * NX + x}

    def along(k, other):
        there = 1 - core if other else core
        return {"rep": rid * 2 + there, "voc": h * NX + lax.rem(x + k, NX)}


    loads = [
        pltpu.make_async_copy(example_hbm, examples, in_sem.at[0]),
        pltpu.make_async_copy(states_hbm, states, in_sem.at[1]),
        pltpu.make_async_copy(weight_hbm, weight, in_sem.at[2]),
        pltpu.make_async_copy(order_hbm, pair_order, in_sem.at[3]),
    ]
    barrier = pltpu.get_barrier_semaphore()

    def greet():
        for k in sorted(range(1, count), key=lambda k: -min(k, count - k)):
            pl.semaphore_signal(
                barrier,
                inc=1,
                device_id={"rep": lax.rem(rid + k, count) * 2 + core},
                device_id_type=MESH,
            )

        pl.semaphore_signal(barrier, inc=1, device_id=pair, device_id_type=MESH)
        for k in range(1, NX):
            for other in range(2):
                pl.semaphore_signal(
                    barrier, inc=1, device_id=along(k, other), device_id_type=MESH
                )
        pl.semaphore_signal(barrier, inc=1, device_id=across, device_id_type=MESH)

    def order():
        ids = lax.broadcasted_iota(jnp.int32, (rows, rows), 0)
        for m in range(mb):
            row = examples[m, pl.ds(rid, 1), :]
            onehot[m] = (ids == row).astype(BF16)
            ordered[m] = jnp.dot(onehot[m], states[m], preferred_element_type=F32).astype(BF16)

    def partials(side, target):
        left = []
        for q in range(chunks):
            g, off, n = PLAN[q]
            at = pl.multiple_of(first[g] + side * gs[g] + off, n)
            left.append(ordered[micro[g], pl.ds(at, n), :])
        left = jnp.concatenate(left, axis=0)

        for j in range(4):
            cols = pl.ds(j * (vocab // 4), vocab // 4)
            target[:, cols] = jnp.dot(left, weight[:, cols], preferred_element_type=F32)

    def pair_copies(q):
        parts = 2 if q == 0 else 1
        wide = vocab // parts
        copies = []
        for p in range(parts):
            at = (pl.ds(base[q], srows[q]), pl.ds(p * wide, wide))
            sem = chunks if p else q
            copies.append(
                pltpu.make_async_remote_copy(
                    src_ref=sent.at[at],
                    dst_ref=got.at[at],
                    send_sem=pair_send.at[sem],
                    recv_sem=pair_recv.at[sem],
                    device_id=pair,
                    device_id_type=MESH,
                )
            )
        return copies

    def send(r, src, dst, send_sem, recv_sem):
        pltpu.make_async_remote_copy(
            src_ref=src,
            dst_ref=dst,
            send_sem=send_sem,
            recv_sem=recv_sem,
            device_id={"rep": r * 2 + core},
            device_id_type=MESH,
        ).start()

    def settle(q):
        rn, cg, per = rows_n[q], cgs[q], cols_n[q] // 4
        at = pl.ds(base[q], srows[q])

        copies = pair_copies(q)
        for p, copy in enumerate(copies):
            copy.wait_recv()

            @pl.loop(p * 4 // len(copies), (p + 1) * 4 // len(copies))
            def _(j):
                cols = pl.ds(pl.multiple_of(j * (vocab // 4), vocab // 4), vocab // 4)
                both = (mine[at, cols] + got[at, cols]).astype(BF16)
                for i in range(per):
                    piece = both[:, i * cg : (i + 1) * cg].reshape(rn, TALL, cg)
                    logits[q][pl.ds((j * per + i) * rn, rn)] = piece

        @pl.loop(1, count)
        def _(k):
            r = lax.rem(rid + k, count)
            send(r, logits[q].at[r], pools[q].at[rid], one_send.at[q], one_recv.at[q])

        pltpu.make_async_copy(logits[q].at[rid], pools[q].at[rid], one_recv.at[q]).start()

    def tables():
        loads[3].wait()
        for m in range(mb):

            @pl.loop(0, count)
            def _(r):
                found = jnp.int32(0)
                for k in range(count):
                    found += jnp.where(pair_order[m, k] == r, pair_order[m, (k + 1) % count], 0)
                partner[m, r] = found

    def turn():
        for m in range(mb):
            ordered_t[:, m * rows : (m + 1) * rows] = ordered[m].T

        @pl.loop(0, 4)
        def _(j):
            at = pl.multiple_of(j * (vocab // 4), vocab // 4)
            weight_t[core, pl.ds(at, vocab // 4), :] = weight[:, pl.ds(at, vocab // 4)].T

    def compare(q):
        pool, batch = pools[q], 8

        def differ(r):
            own, other = pool[r], pool[partner[micro[PLAN[q][0]], r]]
            spread[q][r] = (SCALE * (own.astype(F32) - other.astype(F32))).astype(BF16)

        @pl.loop(0, count // batch)
        def _(b):
            for i in range(batch):
                differ(lax.rem(rid + 1 + b * batch + i, count))
            for i in range(batch - 1):
                r = lax.rem(rid + 1 + b * batch + i, count)
                send(r, spread[q].at[r], grad[q].at[core, rid], two_send.at[q], two_recv.at[q])

            @pl.when(b < count // batch - 1)
            def _():
                r = lax.rem(rid + 1 + b * batch + batch - 1, count)
                send(r, spread[q].at[r], grad[q].at[core, rid], two_send.at[q], two_recv.at[q])

        pltpu.make_async_copy(spread[q].at[rid], grad[q].at[core, rid], two_recv.at[q]).start()

    def await_ref(ref, sem):
        pltpu.make_async_copy(ref, ref, sem).wait()

    def forward(q):
        return pltpu.make_async_remote_copy(
            src_ref=grad[q].at[core],
            dst_ref=grad[q].at[core],
            send_sem=fwd_send.at[q],
            recv_sem=fwd_recv.at[q],
            device_id=pair,
            device_id_type=MESH,
        )

    def turned():
        return pltpu.make_async_remote_copy(
            src_ref=weight_t.at[core],
            dst_ref=weight_t.at[core],
            send_sem=turn_sem.at[0],
            recv_sem=turn_sem.at[1],
            device_id=pair,
            device_id_type=MESH,
        )

    def scatter(q, k):
        return pltpu.make_async_remote_copy(
            src_ref=part_b[q].at[lax.rem(x + k, NX)],
            dst_ref=xin[q].at[x],
            send_sem=xs_send.at[q],
            recv_sem=xs_recv.at[q],
            device_id=along(k, 0),
            device_id_type=MESH,
        )

    def gather(q):
        dst = total[q].at[core * NX + x]
        for k in sorted(range(NX), key=lambda k: -min(k, NX - k)):
            for other in range(2):
                if k or other:
                    pltpu.make_async_remote_copy(
                        src_ref=final[q].at[1 - core if other else core],
                        dst_ref=dst,
                        send_sem=xg_send.at[q],
                        recv_sem=xg_recv.at[q],
                        device_id=along(k, other),
                        device_id_type=MESH,
                    ).start()
        total[q][core * NX + x] = final[q][core]

    def cross(q):
        return pltpu.make_async_remote_copy(
            src_ref=half[q],
            dst_ref=half_in[q],
            send_sem=y_send.at[q],
            recv_sem=y_recv.at[q],
            device_id=across,
            device_id_type=MESH,
        )

    def others(ref, sem):
        few = ref.at[pl.ds(0, ref.shape[0] - 1)]
        pltpu.make_async_copy(few, few, sem).wait()

    def state_part(g):
        lhs = [
            jnp.concatenate(
                [
                    grad[q][core, pl.ds(j * rows_n[q], rows_n[q])].reshape(srows[q], cgs[q])
                    for j in range(cols_n[q])
                ],
                axis=1,
            )
            for q in of[g]
        ]
        lhs = jnp.concatenate(lhs, axis=0)
        for w in range(2):
            out = jnp.dot(lhs, weight_t[w], preferred_element_type=F32)
            part[g][w] = out
            part_b[g][:, w] = out.reshape(NX, quarter[g], width).astype(BF16)

    def head():
        parts = min(8, min(cols_n))
        wide = vocab // parts
        for j in range(parts):
            cols = pl.ds(j * wide, wide)
            right = []
            for g in range(groups):
                for side in range(2):
                    for q in of[g]:
                        per, rn = cols_n[q] // parts, rows_n[q]
                        pieces = [
                            grad[q][side, pl.ds((j * per + i) * rn, rn)].reshape(srows[q], cgs[q])
                            for i in range(per)
                        ]
                        right.append(jnp.concatenate(pieces, axis=1))
            right = jnp.concatenate(right, axis=0)
            out = jnp.dot(ordered_t[...], right, preferred_element_type=F32)
            head_out[:, cols] = out.astype(BF16)
            pltpu.make_async_copy(head_out.at[:, cols], head_hbm.at[:, cols], out_sem.at[0]).start()

    def sum_x(q):
        acc = part[q][:, pl.ds(pl.multiple_of(x * quarter[q], quarter[q]), quarter[q]), :]
        for k in range(1, NX):
            acc += xin[q][lax.rem(x + k, NX)].astype(F32)
        half[q][...] = acc.astype(BF16)

    def sum_h(q):
        final[q][...] = (half[q][...].astype(F32) + half_in[q][...].astype(F32)).astype(BF16)

    def restore(m):
        rows_of = [
            total[g][...].astype(F32).reshape(2 * gs[g], width).astype(BF16)
            for g in range(groups)
            if micro[g] == m
        ]
        state_out[m] = lax.dot_general(
            onehot[m],
            jnp.concatenate(rows_of, axis=0),
            (((0,), (0,)), ((), ())),
            preferred_element_type=F32,
        ).astype(BF16)
        pltpu.make_async_copy(state_out.at[m], state_hbm.at[m], out_sem.at[1]).start()

    def x_stage(q):
        with scope(f"xs_wait{q}"):
            others(xin[q], xs_recv.at[q])
        sum_x(q)
        cross(q).start()

    def y_stage(q):
        with scope(f"y_wait{q}"):
            cross(q).wait_recv()
        sum_h(q)
        gather(q)

    def done(q):
        with scope(f"xg_wait{q}"):
            others(total[q], xg_recv.at[q])

    for load in loads:
        load.start()
    with scope("greet"):
        greet()
    with scope("load"):
        loads[0].wait()
        loads[1].wait()
    with scope("order"):
        order()
    with scope("loadw"):
        loads[2].wait()
    with scope("partial0"):
        partials(1 - core, sent)
    with scope("partial1"):
        partials(core, mine)
    with scope("barrier"):
        pl.semaphore_wait(barrier, count - 1 + 1 + 2 * (NX - 1) + 1)
    for q in range(chunks):
        for copy in pair_copies(q):
            copy.start()
    for q in range(chunks):
        with scope(f"settle{q}"):
            settle(q)
    with scope("turn"):
        turn()
    turned().start()
    with scope("tables"):
        tables()
    for q in range(chunks):
        with scope(f"wait1_{q}"):
            await_ref(pools[q], one_recv.at[q])
        with scope(f"compare{q}"):
            compare(q)
    turned().wait_recv()
    for g in range(groups):
        for q in of[g]:
            with scope(f"wait2_{q}"):
                await_ref(grad[q].at[core], two_recv.at[q])
            forward(q).start()
        with scope(f"state_part{g}"):
            state_part(g)
        for k in sorted(range(1, NX), key=lambda k: -min(k, NX - k)):
            scatter(g, k).start()
        if g > 0:
            x_stage(g - 1)
        if g > 2:
            y_stage(g - 3)
    x_stage(groups - 1)
    y_stage(groups - 3)
    with scope("fwd_wait"):
        for q in range(chunks):
            forward(q).wait_recv()
    with scope("head"):
        head()
    y_stage(groups - 2)
    y_stage(groups - 1)
    for m in range(mb):
        for g in range(groups):
            if micro[g] == m:
                done(g)
        with scope(f"restore{m}"):
            restore(m)

    with scope("drain"):
        turned().wait_send()
        for q in range(chunks):
            for copy in pair_copies(q):
                copy.wait_send()
            others(logits[q], one_send.at[q])
            others(spread[q], two_send.at[q])
            forward(q).wait_send()
        for g in range(groups):
            others(part_b[g], xs_send.at[g])
            others(total[g], xg_send.at[g])
            cross(g).wait_send()
        pltpu.make_async_copy(head_out, head_hbm, out_sem.at[0]).wait()
        pltpu.make_async_copy(state_out, state_hbm, out_sem.at[1]).wait()


def finish(state_in, head_in, state_out, head_out, state, head, in_sem, out_sem):
    pieces = 4
    step = head.shape[0] // pieces
    moves = []
    for p in range(pieces):
        at = pl.ds(p * step, step)
        moves.append((head_in.at[at], head.at[at], head_out.at[at]))
    for m in range(state.shape[0]):
        moves.append((state_in.at[m], state.at[m], state_out.at[m]))
    ins = [pltpu.make_async_copy(a, b, in_sem.at[i]) for i, (a, b, _) in enumerate(moves)]
    outs = [pltpu.make_async_copy(b, c, out_sem.at[i]) for i, (_, b, c) in enumerate(moves)]
    for copy in ins:
        copy.start()
    for copy_in, copy_out in zip(ins, outs):
        copy_in.wait()
        copy_out.start()
    for copy in outs:
        copy.wait()


def build(mesh, dims):
    NZ, NY, NX, NH = dims

    def body(states, head_weight, pair_order, row_example):
        mb, rows, width = states.shape
        vocab = head_weight.shape[1]
        count = NZ * NY
        chunks = len(PLAN)
        groups = len(GROUPS)
        srows = [n for _, _, n in PLAN]
        gs = [sum(ns) for _, ns in GROUPS]
        slots = [(count, TALL, vocab * n // (count * TALL)) for n in srows]
        quarter = [n // NX for n in gs]
        vm = pltpu.VMEM
        dma = pltpu.SemaphoreType.DMA
        hbm = pl.BlockSpec(memory_space=pl.ANY)
        shapes = (
            jax.ShapeDtypeStruct(states.shape, BF16),
            jax.ShapeDtypeStruct(head_weight.shape, BF16),
        )
        made = pl.pallas_call(
            functools.partial(kernel, dims),
            out_shape=shapes,
            in_specs=[hbm, hbm, hbm, hbm],
            out_specs=(hbm, hbm),
            scratch_shapes=[
                pltpu.SMEM((mb, count), jnp.int32),
                vm((width, vocab), BF16),
                vm((2, vocab, width), BF16),
                vm((mb, rows, width), BF16),
                vm(row_example.shape, jnp.int32),
                vm((mb, rows, rows), BF16),
                vm((mb, rows, width), BF16),
                vm((width, mb * rows), BF16),
                vm((sum(srows), vocab), F32),
                vm((sum(srows), vocab), F32),
                vm((sum(srows), vocab), F32),
                [vm(slot, BF16) for slot in slots],
                [vm(slot, BF16) for slot in slots],
                [vm(slot, BF16) for slot in slots],
                [vm((2, *slot), BF16) for slot in slots],
                [vm((2, n, width), F32) for n in gs],
                [vm((NX, 2, n, width), BF16) for n in quarter],
                [vm((NX, 2, n, width), BF16) for n in quarter],
                [vm((2, n, width), BF16) for n in quarter],
                [vm((2, n, width), BF16) for n in quarter],
                [vm((2, n, width), BF16) for n in quarter],
                [vm((2 * NX, n, width), BF16) for n in quarter],
                vm((mb, rows, width), BF16),
                vm((width, vocab), BF16),
                pltpu.SMEM((mb, count), jnp.int32),
                dma((4,)),
                dma((2,)),
            ]
            + [dma((chunks + 1,))] * 2
            + [dma((chunks,))] * 6
            + [dma((2,))]
            + [dma((groups,))] * 6,
            compiler_params=pltpu.CompilerParams(
                collective_id=0, has_side_effects=True, vmem_limit_bytes=60 * 1024 * 1024
            ),
        )(pair_order, states, head_weight, row_example)
        pieces = 4 + mb
        return pl.pallas_call(
            finish,
            out_shape=shapes,
            in_specs=[hbm, hbm],
            out_specs=(hbm, hbm),
            scratch_shapes=[
                vm(states.shape, BF16),
                vm(head_weight.shape, BF16),
                dma((pieces,)),
                dma((pieces,)),
            ],
            compiler_params=pltpu.CompilerParams(vmem_limit_bytes=60 * 1024 * 1024),
        )(*made)

    return jax.shard_map(
        body,
        mesh=mesh,
        in_specs=(P(None, None, "rep"), P("rep", "voc"), P(), P()),
        out_specs=(P(None, None, "rep"), P("rep", "voc")),
        check_vma=False,
    )


def solution(mesh):
    return build(mesh, (8, 4, 4, 2))
```

```python
import functools

import jax
import jax.numpy as jnp
from jax import lax
from jax.experimental import pallas as pl
from jax.experimental.pallas import tpu as pltpu
from jax.sharding import PartitionSpec as P

MESH = pl.DeviceIdType.MESH
SCALE = 0.0625
GROUPS = ((0, (32, 32)), (0, (64,)), (1, (64,)), (1, (64,)))
PLAN = [(g, sum(ns[:i]), n) for g, (_, ns) in enumerate(GROUPS) for i, n in enumerate(ns)]
TALL = 16
F32, BF16 = jnp.float32, jnp.bfloat16
scope = jax.named_scope


def kernel(
    dims,
    order_hbm,
    states_hbm,
    weight_hbm,
    example_hbm,
    state_hbm,
    head_hbm,
    pair_order,
    weight,
    weight_t,
    states,
    examples,
    onehot,
    ordered,
    ordered_t,
    mine,
    sent,
    got,
    logits,
    pools,
    spread,
    grad,
    part,
    part_b,
    xin,
    half,
    half_in,
    final,
    total,
    state_out,
    head_out,
    partner,
    in_sem,
    out_sem,
    pair_send,
    pair_recv,
    one_send,
    one_recv,
    two_send,
    two_recv,
    fwd_send,
    fwd_recv,
    turn_sem,
    xs_send,
    xs_recv,
    y_send,
    y_recv,
    xg_send,
    xg_recv,
):
    NZ, NY, NX, NH = dims
    mb, rows, width = states.shape
    vocab = weight.shape[1]
    count = NZ * NY
    chunks = len(PLAN)
    groups = len(GROUPS)
    micro = [m for m, _ in GROUPS]
    gs = [sum(ns) for _, ns in GROUPS]
    first = [2 * sum(n for p, n in zip(micro[:g], gs) if p == micro[g]) for g in range(groups)]
    of = [[q for q in range(chunks) if PLAN[q][0] == g] for g in range(groups)]
    srows = [n for _, _, n in PLAN]
    base = [sum(srows[:q]) for q in range(chunks)]
    rows_n = [n // TALL for n in srows]
    cols_n = [count // n for n in rows_n]
    cgs = [vocab // n for n in cols_n]
    quarter = [n // NX for n in gs]

    rep, voc = lax.axis_index("rep"), lax.axis_index("voc")
    core = lax.rem(rep, 2)
    rid = rep // 2
    z, y = rid // NY, lax.rem(rid, NY)
    h, x = voc // NX, lax.rem(voc, NX)
    pair = {"rep": rid * 2 + 1 - core}
    across = {"voc": (NH - 1 - h) * NX + x}

    def along(k, other):
        there = 1 - core if other else core
        return {"rep": rid * 2 + there, "voc": h * NX + lax.rem(x + k, NX)}


    loads = [
        pltpu.make_async_copy(example_hbm, examples, in_sem.at[0]),
        pltpu.make_async_copy(states_hbm, states, in_sem.at[1]),
        pltpu.make_async_copy(weight_hbm, weight, in_sem.at[2]),
        pltpu.make_async_copy(order_hbm, pair_order, in_sem.at[3]),
    ]
    barrier = pltpu.get_barrier_semaphore()

    def greet():
        for k in sorted(range(1, count), key=lambda k: -min(k, count - k)):
            pl.semaphore_signal(
                barrier,
                inc=1,
                device_id={"rep": lax.rem(rid + k, count) * 2 + core},
                device_id_type=MESH,
            )

        pl.semaphore_signal(barrier, inc=1, device_id=pair, device_id_type=MESH)
        for k in range(1, NX):
            for other in range(2):
                pl.semaphore_signal(
                    barrier, inc=1, device_id=along(k, other), device_id_type=MESH
                )
        pl.semaphore_signal(barrier, inc=1, device_id=across, device_id_type=MESH)

    def order():
        ids = lax.broadcasted_iota(jnp.int32, (rows, rows), 0)
        for m in range(mb):
            row = examples[m, pl.ds(rid, 1), :]
            onehot[m] = (ids == row).astype(BF16)
            ordered[m] = jnp.dot(onehot[m], states[m], preferred_element_type=F32).astype(BF16)

    def partials(side, target):
        left = []
        for q in range(chunks):
            g, off, n = PLAN[q]
            at = pl.multiple_of(first[g] + side * gs[g] + off, n)
            left.append(ordered[micro[g], pl.ds(at, n), :])
        left = jnp.concatenate(left, axis=0)

        for j in range(4):
            cols = pl.ds(j * (vocab // 4), vocab // 4)
            target[:, cols] = jnp.dot(left, weight[:, cols], preferred_element_type=F32)

    def pair_copies(q):
        parts = 2 if q == 0 else 1
        wide = vocab // parts
        copies = []
        for p in range(parts):
            at = (pl.ds(base[q], srows[q]), pl.ds(p * wide, wide))
            sem = chunks if p else q
            copies.append(
                pltpu.make_async_remote_copy(
                    src_ref=sent.at[at],
                    dst_ref=got.at[at],
                    send_sem=pair_send.at[sem],
                    recv_sem=pair_recv.at[sem],
                    device_id=pair,
                    device_id_type=MESH,
                )
            )
        return copies

    def send(r, src, dst, send_sem, recv_sem):
        pltpu.make_async_remote_copy(
            src_ref=src,
            dst_ref=dst,
            send_sem=send_sem,
            recv_sem=recv_sem,
            device_id={"rep": r * 2 + core},
            device_id_type=MESH,
        ).start()

    def settle(q):
        rn, cg, per = rows_n[q], cgs[q], cols_n[q] // 4
        at = pl.ds(base[q], srows[q])

        copies = pair_copies(q)
        for p, copy in enumerate(copies):
            copy.wait_recv()

            for j in range(p * 4 // len(copies), (p + 1) * 4 // len(copies)):
                cols = pl.ds(j * (vocab // 4), vocab // 4)
                both = (mine[at, cols] + got[at, cols]).astype(BF16)
                for i in range(per):
                    piece = both[:, i * cg : (i + 1) * cg].reshape(rn, TALL, cg)
                    logits[q][pl.ds((j * per + i) * rn, rn)] = piece

        @pl.loop(1, count)
        def _(k):
            r = lax.rem(rid + k, count)
            send(r, logits[q].at[r], pools[q].at[rid], one_send.at[q], one_recv.at[q])

        pltpu.make_async_copy(logits[q].at[rid], pools[q].at[rid], one_recv.at[q]).start()

    def tables():
        loads[3].wait()
        for m in range(mb):

            @pl.loop(0, count)
            def _(r):
                found = jnp.int32(0)
                for k in range(count):
                    found += jnp.where(pair_order[m, k] == r, pair_order[m, (k + 1) % count], 0)
                partner[m, r] = found

    def turn():
        for m in range(mb):
            ordered_t[:, m * rows : (m + 1) * rows] = ordered[m].T

        @pl.loop(0, 4)
        def _(j):
            at = pl.multiple_of(j * (vocab // 4), vocab // 4)
            weight_t[core, pl.ds(at, vocab // 4), :] = weight[:, pl.ds(at, vocab // 4)].T

    def compare(q):
        pool, batch = pools[q], 8

        def differ(r):
            own, other = pool[r], pool[partner[micro[PLAN[q][0]], r]]
            spread[q][r] = (SCALE * (own.astype(F32) - other.astype(F32))).astype(BF16)

        @pl.loop(0, count // batch)
        def _(b):
            for i in range(batch):
                differ(lax.rem(rid + 1 + b * batch + i, count))
            for i in range(batch - 1):
                r = lax.rem(rid + 1 + b * batch + i, count)
                send(r, spread[q].at[r], grad[q].at[core, rid], two_send.at[q], two_recv.at[q])

            @pl.when(b < count // batch - 1)
            def _():
                r = lax.rem(rid + 1 + b * batch + batch - 1, count)
                send(r, spread[q].at[r], grad[q].at[core, rid], two_send.at[q], two_recv.at[q])

        pltpu.make_async_copy(spread[q].at[rid], grad[q].at[core, rid], two_recv.at[q]).start()

    def await_ref(ref, sem):
        pltpu.make_async_copy(ref, ref, sem).wait()

    def forward(q):
        return pltpu.make_async_remote_copy(
            src_ref=grad[q].at[core],
            dst_ref=grad[q].at[core],
            send_sem=fwd_send.at[q],
            recv_sem=fwd_recv.at[q],
            device_id=pair,
            device_id_type=MESH,
        )

    def turned():
        return pltpu.make_async_remote_copy(
            src_ref=weight_t.at[core],
            dst_ref=weight_t.at[core],
            send_sem=turn_sem.at[0],
            recv_sem=turn_sem.at[1],
            device_id=pair,
            device_id_type=MESH,
        )

    def scatter(q, k):
        return pltpu.make_async_remote_copy(
            src_ref=part_b[q].at[lax.rem(x + k, NX)],
            dst_ref=xin[q].at[x],
            send_sem=xs_send.at[q],
            recv_sem=xs_recv.at[q],
            device_id=along(k, 0),
            device_id_type=MESH,
        )

    def gather(q):
        dst = total[q].at[core * NX + x]
        for k in sorted(range(NX), key=lambda k: -min(k, NX - k)):
            for other in range(2):
                if k or other:
                    pltpu.make_async_remote_copy(
                        src_ref=final[q].at[1 - core if other else core],
                        dst_ref=dst,
                        send_sem=xg_send.at[q],
                        recv_sem=xg_recv.at[q],
                        device_id=along(k, other),
                        device_id_type=MESH,
                    ).start()
        total[q][core * NX + x] = final[q][core]

    def cross(q):
        return pltpu.make_async_remote_copy(
            src_ref=half[q],
            dst_ref=half_in[q],
            send_sem=y_send.at[q],
            recv_sem=y_recv.at[q],
            device_id=across,
            device_id_type=MESH,
        )

    def others(ref, sem):
        few = ref.at[pl.ds(0, ref.shape[0] - 1)]
        pltpu.make_async_copy(few, few, sem).wait()

    def state_part(g):
        lhs = [
            jnp.concatenate(
                [
                    grad[q][core, pl.ds(j * rows_n[q], rows_n[q])].reshape(srows[q], cgs[q])
                    for j in range(cols_n[q])
                ],
                axis=1,
            )
            for q in of[g]
        ]
        lhs = jnp.concatenate(lhs, axis=0)
        for w in range(2):
            out = jnp.dot(lhs, weight_t[w], preferred_element_type=F32)
            part[g][w] = out
            part_b[g][:, w] = out.reshape(NX, quarter[g], width).astype(BF16)

    def head():
        parts = min(8, min(cols_n))
        wide = vocab // parts
        for j in range(parts):
            cols = pl.ds(j * wide, wide)
            right = []
            for g in range(groups):
                for side in range(2):
                    for q in of[g]:
                        per, rn = cols_n[q] // parts, rows_n[q]
                        pieces = [
                            grad[q][side, pl.ds((j * per + i) * rn, rn)].reshape(srows[q], cgs[q])
                            for i in range(per)
                        ]
                        right.append(jnp.concatenate(pieces, axis=1))
            right = jnp.concatenate(right, axis=0)
            out = jnp.dot(ordered_t[...], right, preferred_element_type=F32)
            head_out[:, cols] = out.astype(BF16)
            pltpu.make_async_copy(head_out.at[:, cols], head_hbm.at[:, cols], out_sem.at[0]).start()

    def sum_x(q):
        acc = part[q][:, pl.ds(pl.multiple_of(x * quarter[q], quarter[q]), quarter[q]), :]
        for k in range(1, NX):
            acc += xin[q][lax.rem(x + k, NX)].astype(F32)
        half[q][...] = acc.astype(BF16)

    def sum_h(q):
        final[q][...] = (half[q][...].astype(F32) + half_in[q][...].astype(F32)).astype(BF16)

    def restore(m):
        rows_of = [
            total[g][...].astype(F32).reshape(2 * gs[g], width).astype(BF16)
            for g in range(groups)
            if micro[g] == m
        ]
        state_out[m] = lax.dot_general(
            onehot[m],
            jnp.concatenate(rows_of, axis=0),
            (((0,), (0,)), ((), ())),
            preferred_element_type=F32,
        ).astype(BF16)
        pltpu.make_async_copy(state_out.at[m], state_hbm.at[m], out_sem.at[1]).start()

    def x_stage(q):
        with scope(f"xs_wait{q}"):
            others(xin[q], xs_recv.at[q])
        sum_x(q)
        cross(q).start()

    def y_stage(q):
        with scope(f"y_wait{q}"):
            cross(q).wait_recv()
        sum_h(q)
        gather(q)

    def done(q):
        with scope(f"xg_wait{q}"):
            others(total[q], xg_recv.at[q])

    for load in loads:
        load.start()
    with scope("greet"):
        greet()
    with scope("load"):
        loads[0].wait()
        loads[1].wait()
    with scope("order"):
        order()
    with scope("loadw"):
        loads[2].wait()
    with scope("partial0"):
        partials(1 - core, sent)
    with scope("partial1"):
        partials(core, mine)
    with scope("barrier"):
        pl.semaphore_wait(barrier, count - 1 + 1 + 2 * (NX - 1) + 1)
    for q in range(chunks):
        for copy in pair_copies(q):
            copy.start()
    for q in range(chunks):
        with scope(f"settle{q}"):
            settle(q)
    with scope("turn"):
        turn()
    turned().start()
    with scope("tables"):
        tables()
    for q in range(chunks):
        with scope(f"wait1_{q}"):
            await_ref(pools[q], one_recv.at[q])
        with scope(f"compare{q}"):
            compare(q)
    turned().wait_recv()
    for g in range(groups):
        for q in of[g]:
            with scope(f"wait2_{q}"):
                await_ref(grad[q].at[core], two_recv.at[q])
            forward(q).start()
        with scope(f"state_part{g}"):
            state_part(g)
        for k in sorted(range(1, NX), key=lambda k: -min(k, NX - k)):
            scatter(g, k).start()
        if g > 0:
            x_stage(g - 1)
        if g > 2:
            y_stage(g - 3)
    x_stage(groups - 1)
    y_stage(groups - 3)
    with scope("fwd_wait"):
        for q in range(chunks):
            forward(q).wait_recv()
    with scope("head"):
        head()
    y_stage(groups - 2)
    y_stage(groups - 1)
    for m in range(mb):
        for g in range(groups):
            if micro[g] == m:
                done(g)
        with scope(f"restore{m}"):
            restore(m)

    with scope("drain"):
        turned().wait_send()
        for q in range(chunks):
            for copy in pair_copies(q):
                copy.wait_send()
            others(logits[q], one_send.at[q])
            others(spread[q], two_send.at[q])
            forward(q).wait_send()
        for g in range(groups):
            others(part_b[g], xs_send.at[g])
            others(total[g], xg_send.at[g])
            cross(g).wait_send()
        pltpu.make_async_copy(head_out, head_hbm, out_sem.at[0]).wait()
        pltpu.make_async_copy(state_out, state_hbm, out_sem.at[1]).wait()


def finish(state_in, head_in, state_out, head_out, state, head, in_sem, out_sem):
    pieces = 4
    step = head.shape[0] // pieces
    moves = []
    for p in range(pieces):
        at = pl.ds(p * step, step)
        moves.append((head_in.at[at], head.at[at], head_out.at[at]))
    for m in range(state.shape[0]):
        moves.append((state_in.at[m], state.at[m], state_out.at[m]))
    ins = [pltpu.make_async_copy(a, b, in_sem.at[i]) for i, (a, b, _) in enumerate(moves)]
    outs = [pltpu.make_async_copy(b, c, out_sem.at[i]) for i, (_, b, c) in enumerate(moves)]
    for copy in ins:
        copy.start()
    for copy_in, copy_out in zip(ins, outs):
        copy_in.wait()
        copy_out.start()
    for copy in outs:
        copy.wait()


def build(mesh, dims):
    NZ, NY, NX, NH = dims

    def body(states, head_weight, pair_order, row_example):
        mb, rows, width = states.shape
        vocab = head_weight.shape[1]
        count = NZ * NY
        chunks = len(PLAN)
        groups = len(GROUPS)
        srows = [n for _, _, n in PLAN]
        gs = [sum(ns) for _, ns in GROUPS]
        slots = [(count, TALL, vocab * n // (count * TALL)) for n in srows]
        quarter = [n // NX for n in gs]
        vm = pltpu.VMEM
        dma = pltpu.SemaphoreType.DMA
        hbm = pl.BlockSpec(memory_space=pl.ANY)
        shapes = (
            jax.ShapeDtypeStruct(states.shape, BF16),
            jax.ShapeDtypeStruct(head_weight.shape, BF16),
        )
        made = pl.pallas_call(
            functools.partial(kernel, dims),
            out_shape=shapes,
            in_specs=[hbm, hbm, hbm, hbm],
            out_specs=(hbm, hbm),
            scratch_shapes=[
                pltpu.SMEM((mb, count), jnp.int32),
                vm((width, vocab), BF16),
                vm((2, vocab, width), BF16),
                vm((mb, rows, width), BF16),
                vm(row_example.shape, jnp.int32),
                vm((mb, rows, rows), BF16),
                vm((mb, rows, width), BF16),
                vm((width, mb * rows), BF16),
                vm((sum(srows), vocab), F32),
                vm((sum(srows), vocab), F32),
                vm((sum(srows), vocab), F32),
                [vm(slot, BF16) for slot in slots],
                [vm(slot, BF16) for slot in slots],
                [vm(slot, BF16) for slot in slots],
                [vm((2, *slot), BF16) for slot in slots],
                [vm((2, n, width), F32) for n in gs],
                [vm((NX, 2, n, width), BF16) for n in quarter],
                [vm((NX, 2, n, width), BF16) for n in quarter],
                [vm((2, n, width), BF16) for n in quarter],
                [vm((2, n, width), BF16) for n in quarter],
                [vm((2, n, width), BF16) for n in quarter],
                [vm((2 * NX, n, width), BF16) for n in quarter],
                vm((mb, rows, width), BF16),
                vm((width, vocab), BF16),
                pltpu.SMEM((mb, count), jnp.int32),
                dma((4,)),
                dma((2,)),
            ]
            + [dma((chunks + 1,))] * 2
            + [dma((chunks,))] * 6
            + [dma((2,))]
            + [dma((groups,))] * 6,
            compiler_params=pltpu.CompilerParams(
                collective_id=0, has_side_effects=True, vmem_limit_bytes=60 * 1024 * 1024
            ),
        )(pair_order, states, head_weight, row_example)
        pieces = 4 + mb
        return pl.pallas_call(
            finish,
            out_shape=shapes,
            in_specs=[hbm, hbm],
            out_specs=(hbm, hbm),
            scratch_shapes=[
                vm(states.shape, BF16),
                vm(head_weight.shape, BF16),
                dma((pieces,)),
                dma((pieces,)),
            ],
            compiler_params=pltpu.CompilerParams(vmem_limit_bytes=60 * 1024 * 1024),
        )(*made)

    return jax.shard_map(
        body,
        mesh=mesh,
        in_specs=(P(None, None, "rep"), P("rep", "voc"), P(), P()),
        out_specs=(P(None, None, "rep"), P("rep", "voc")),
        check_vma=False,
    )


def solution(mesh):
    return build(mesh, (8, 4, 4, 2))
```
